32 devices in a mesh: batch: 4 (over x, core), centers: 8 (over z, y).
Axes of the slice: x: 2, y: 2, z: 4, core: 2. Of those that a mesh axis runs over, the one named last changes fastest.
Arguments:
- pool_features: float32 [32768, 128], P(('batch', 'centers')), may hold values from -14 to 14
- pool_targets: float32 [32768, 64], P(('batch', 'centers')), may hold values from -6 to 6
- batch_index: int32 [2048], P(('batch', 'centers')), may hold values from 0 to 1023
- centers: float32 [4096, 128], P('centers'), may hold values from -14 to 14
- weights: float32 [4096, 64], P('centers'), as said below
- eig_vectors: float32 [4096, 1024], P(('batch', 'centers')), may hold values from -0.09375 to 0.09375
- eig_scale: float32 [1024], replicated, may hold values from 0.5 to 4
- nys_owner: int32 [4096, 1], P(('batch', 'centers')), may hold values from 0 to 7; in each aligned block of 128 rows (0 to 127, 128 to 255, ...) at most 32 rows name the same one
- nys_offset: int32 [4096], P(('batch', 'centers')), may hold values from 0 to 511
Outputs:
- residual_out: float32 [2048, 64], P(('batch', 'centers'))
- update: float32 [4096, 64], P('centers')
The draws below stay inside these ranges and needn't reach their ends.
Inputs may be any that keep to these rules, and one draw needn't show every extreme that they name: `nys_owner`: among the 128 rows of one device no owner is named more than 32 times; on some devices one owner is named exactly 32 times. `weights`: every column sums to zero.
All inputs are finite; a program needn't handle non-finite values.
Results may differ from the reference program's by a relative error of at most 0.0003.
Values sent between devices are 32-bit elements; how exact they have to be, the bound alone decides.
A program may use at most 64 MiB of HBM per device.

```python
import math
import jax
import jax.numpy as jnp
import numpy as np
from jax import lax

D = 128
OUT = 64
Q = 1024
DEPTH = 3
NYS_DEV = 128
POOL_DEV = 1024
ROWS_LOC = 64
CDEV = 512
CAP = 32
M = 2048
P_SIZE = 4096
S = 4096
POOL = 32768
N_CENTERS = 8


def cluster_means(key):
    means = jax.random.truncated_normal(jax.random.fold_in(key, 101), -4.0, 4.0, (16, D), jnp.float32)
    return means


def noisy_points(key, count, salt):
    means = cluster_means(key)
    label = jax.random.randint(jax.random.fold_in(key, salt), (count,), 0, means.shape[0])
    level = jnp.exp(jax.random.uniform(jax.random.fold_in(key, salt + 1), (count, 1), jnp.float32, math.log(0.15), math.log(2.0)))
    noise = jax.random.truncated_normal(jax.random.fold_in(key, salt + 2), -4.0, 4.0, (count, D), jnp.float32)
    return means[label] + level * noise


def draw_pool_features(key, part):
    return noisy_points(key, POOL, 301)


def draw_centers(key, part):
    return noisy_points(key, P_SIZE, 401)


def draw_weights(key, part):
    base = jax.random.normal(jax.random.fold_in(key, 501), (P_SIZE, OUT), jnp.float32)
    base = base - jnp.mean(base, axis=0, keepdims=True)
    return base * (0.3 / math.sqrt(P_SIZE))


def set_ends(values, rng, smallest, high):
    longest = values.shape.index(max(values.shape))
    spots = []
    for shift in (0, 1):
        where = [jax.random.randint(jax.random.fold_in(rng, axis), (), 0, length) for axis, length in enumerate(values.shape)]
        where[longest] = (where[longest] + shift) % values.shape[longest]
        spots.append(tuple(where))
    return values.at[spots[0]].set(smallest).at[spots[1]].set(high)


def steps_of(stream_key, extent, shards, low, largest):
    factor_of, own = 1.0, jax.random.fold_in(stream_key, 6)
    for position, blocks in shards:
        draws = jnp.exp(jax.random.uniform(jax.random.fold_in(own, position), (blocks,), jnp.float32, low / len(shards), largest / len(shards)))
        factor_of = factor_of * jnp.repeat(draws, extent[position] // blocks).reshape([-1 if axis == position else 1 for axis in range(len(extent))])
    return factor_of


def routed_block(own_key, own, number, rows, number_of, top, bound, slope):
    sequence = jax.random.permutation(own_key, number_of)
    crowded, common = load_shares(number_of, rows * top, bound, slope, True), load_shares(number_of, rows * top, bound, slope, False)
    places = jnp.arange(number_of)

    def named(lengths, turn):
        used = int((lengths > 0).sum())
        fixed = max(1, used // 4)
        moved = fixed + (places - fixed + turn * (used - fixed)) % max(1, number_of - fixed)
        return jnp.zeros((number_of,), jnp.int32).at[sequence[jnp.where(places < fixed, places, moved)]].set(jnp.asarray(lengths, jnp.int32))

    lengths = jnp.where(number % 4 == 0, named(crowded, number // 4), named(common, number - number // 4 - 1))
    mixed = jax.random.permutation(jax.random.fold_in(own, 3), number_of)
    donor, receiver = mixed[0:number_of // 2 * 2:2], mixed[1:number_of // 2 * 2:2]
    slack = jnp.minimum(lengths[donor] - 1, bound - lengths[receiver]) // 2
    slack = jnp.where((donor == sequence[0]) | (receiver == sequence[0]) | (lengths[receiver] == 0), 0, jnp.maximum(slack, 0))
    moved = jax.random.randint(jax.random.fold_in(own, 4), (number_of // 2,), 0, 1 << 20) % (slack + 1)
    lengths = lengths.at[donor].add(-moved).at[receiver].add(moved)
    members = jnp.searchsorted(jnp.cumsum(lengths), jnp.arange(rows * top), side="right").astype(jnp.int32)
    listing = members.reshape(top, rows).T
    listing = listing[jax.random.permutation(jax.random.fold_in(own, 1), rows)]
    turn = jax.random.randint(jax.random.fold_in(own, 2), (rows, 1), 0, top)
    return jnp.take_along_axis(listing, (jnp.arange(top)[None, :] + turn) % top, axis=1)


def load_shares(number_of, total, reach, lean, full):
    weights = [(1 << 20) // math.isqrt(standing ** lean) + 1 for standing in range(1, number_of + 1)]
    largest = reach if full else min(reach, max(-(-total // number_of), total * weights[0] // sum(weights)))
    least = 1 if total - largest >= number_of - 1 else 0
    holding, surplus = [largest] + [least] * (number_of - 1), total - largest - least * (number_of - 1)
    while surplus > 0:
        movable = [i for i in range(1, number_of) if holding[i] < largest] or [i for i in range(1, number_of) if holding[i] < reach]
        whole, left = sum([weights[i] for i in movable]), surplus
        for i in movable:
            extra = min(reach - holding[i], max(1, left * weights[i] // whole), surplus)
            holding[i] = holding[i] + extra
            surplus = surplus - extra
    return np.array(holding)


def normal_values(stream_key, shape, deviation, bound, cuts=(), kind=jnp.bfloat16):
    values = jax.random.normal(stream_key, shape, jnp.float32) * deviation
    if len(cuts) > 0:
        values = steps_of(stream_key, shape, cuts, -0.22, 0.18) * values
    return jnp.clip(values, min=-bound, max=bound).astype(kind)


def setup_inputs(seed: int = 0) -> dict:
    key_list = jax.random.split(jax.random.key(seed), 10)
    pool_features = draw_pool_features(jax.random.fold_in(key_list[9], 71), 0)
    pool_targets = normal_values(key_list[1], (POOL, OUT), 1.0, 6.0, ((0, 32),), jnp.float32)
    batch_index = set_ends(jax.random.randint(key_list[2], (M,), 0, POOL_DEV), jax.random.fold_in(key_list[2], 1), 0, POOL_DEV - 1).astype(jnp.int32)
    centers = draw_centers(jax.random.fold_in(key_list[9], 71), 0)
    weights = draw_weights(jax.random.fold_in(key_list[9], 71), 0)
    eig_vectors = normal_values(key_list[5], (S, Q), S ** -0.5, 0.09375, ((0, 32),), jnp.float32)
    eig_scale = jnp.clip(jnp.exp(jax.random.uniform(key_list[6], (Q,), jnp.float32, math.log(0.5), math.log(4.0))), 0.5, 4.0)
    nys_owner_keys = jax.random.split(jax.random.fold_in(key_list[7], 1), S // NYS_DEV)
    nys_owner_turns = jax.random.permutation(jax.random.fold_in(key_list[7], 3), S // NYS_DEV)
    nys_owner = jax.vmap(lambda own, number: routed_block(jax.random.fold_in(key_list[7], 2), own, number, NYS_DEV, N_CENTERS, 1, CAP, 2))(nys_owner_keys, nys_owner_turns).reshape((S, 1))
    nys_offset = set_ends(jax.random.randint(key_list[8], (S,), 0, CDEV), jax.random.fold_in(key_list[8], 1), 0, CDEV - 1).astype(jnp.int32)
    return {"pool_features": pool_features, "pool_targets": pool_targets, "batch_index": batch_index, "centers": centers, "weights": weights, "eig_vectors": eig_vectors, "eig_scale": eig_scale, "nys_owner": nys_owner, "nys_offset": nys_offset}


epsilon = 1e-06
highest = lax.Precision.HIGHEST

def kernel_rows(row_block, center_block, center_norm):
    inner_prod = lax.dot_general(row_block, center_block, (((1,), (1,)), ((), ())), precision=highest, preferred_element_type=jnp.float32) / row_block.shape[1]
    row_norm = lax.optimization_barrier(jnp.mean(row_block * row_block, axis=1)) + epsilon
    norm_scale = jnp.sqrt(row_norm[:, None] * center_norm[None, :])
    sigma_now = inner_prod
    tangent = inner_prod
    for depth_step in range(DEPTH):
        cosine = sigma_now / norm_scale
        arc_angle = jnp.arccos(cosine)
        remain = (math.pi - arc_angle) / math.pi
        sigma_now = norm_scale * (jnp.sqrt(1.0 - cosine * cosine) + (math.pi - arc_angle) * cosine) / math.pi
        tangent = sigma_now + tangent * remain
    return tangent

def reference(pool_features, pool_targets, batch_index, centers, weights, eig_vectors, eig_scale, nys_owner, nys_offset):
    rows_total = batch_index.shape[0]
    block_of = jnp.arange(rows_total, dtype=jnp.int32) // ROWS_LOC
    picked = (block_of * POOL_DEV + batch_index).astype(jnp.int32)
    features = pool_features[picked]
    targets = pool_targets[picked]
    center_norm = lax.optimization_barrier(jnp.mean(centers * centers, axis=1)) + epsilon
    block_size = math.gcd(512, rows_total)
    block_count = rows_total // block_size
    feat_blocks = features.reshape(block_count, block_size, features.shape[1])
    targ_blocks = targets.reshape(block_count, block_size, targets.shape[1])

    def step_block(accum, pieces):
        feat, targ = pieces
        kern = kernel_rows(feat, centers, center_norm)
        pred = jnp.dot(kern, weights, precision=highest, preferred_element_type=jnp.float32)
        resid = pred - targ
        accum = accum + lax.dot_general(kern, resid, (((0,), (0,)), ((), ())), precision=highest, preferred_element_type=jnp.float32)
        return (accum, resid)
    total, resid_blocks = lax.scan(step_block, jnp.zeros((centers.shape[0], weights.shape[1]), jnp.float32), (feat_blocks, targ_blocks))
    residual_out = resid_blocks.reshape(rows_total, weights.shape[1])
    grads = total / math.sqrt(rows_total)
    nys = (nys_owner[:, 0] * CDEV + nys_offset).astype(jnp.int32)
    coeff = lax.dot_general(eig_vectors, grads[nys], (((0,), (0,)), ((), ())), precision=highest, preferred_element_type=jnp.float32)
    corr_rows = jnp.dot(eig_vectors, eig_scale[:, None] * coeff, precision=highest, preferred_element_type=jnp.float32)
    correction = jnp.zeros((centers.shape[0], weights.shape[1]), jnp.float32).at[nys].add(corr_rows)
    return (residual_out, correction - grads)
```

```python
import functools
import math

import jax
import jax.numpy as jnp
from jax import lax
from jax.experimental import pallas as pl
from jax.experimental.pallas import tpu as pltpu
from jax.sharding import PartitionSpec as P

DEPTH = 3
EPS = 1e-06
HIGH = lax.Precision.HIGHEST
MESH = pl.DeviceIdType.MESH
ACOS = (
    1.5707963050,
    -0.2145988016,
    0.0889789874,
    -0.0501743046,
    0.0308918810,
    -0.0170881256,
    0.0066700901,
    -0.0012624911,
)


def dot(a, b, ca, cb):
    return lax.dot_general(
        a,
        b,
        (((ca,), (cb,)), ((), ())),
        precision=HIGH,
        preferred_element_type=jnp.float32,
    )


def arc_parts(x):
    u = jnp.maximum(1.0 - x, 1e-30)
    poly = jnp.full_like(x, ACOS[-1] / math.pi)
    for a in ACOS[-2::-1]:
        poly = poly * x + a / math.pi
    v = u * (1.0 + x)
    return u * lax.rsqrt(u) * poly, v * lax.rsqrt(v) * (1.0 / math.pi)


def tangent_kernel(cosine):
    arc, sine = arc_parts(jnp.abs(cosine))
    remain = jnp.where(cosine < 0.0, arc, 1.0 - arc)
    prod = remain * cosine
    sigma = sine + prod
    tangent = sigma + prod
    for _ in range(DEPTH - 1):
        arc, sine = arc_parts(sigma)
        remain = 1.0 - arc
        sigma = sine + remain * sigma
        tangent = sigma + tangent * remain
    return tangent


def body(
    nb,
    nc,
    feat,
    targ,
    cen,
    wts,
    eig,
    scale,
    owner,
    offset,
    res_out,
    upd_out,
    feat_all,
    kbuf,
    ppart,
    prx,
    rsend,
    rrx,
    packed,
    eigrx,
    offsend,
    offrx,
    ebar,
    gsend,
    grx,
    gown,
    gall,
    csend,
    crx,
    cown,
    call,
    usend,
    urx,
    uown,
    uall,
    f_s,
    f_r,
    p_s,
    p_r,
    r_s,
    r_r,
    e_s,
    e_r,
    o_s,
    o_r,
    g_s,
    g_r,
    ga_s,
    ga_r,
    c_s,
    c_r,
    ca_s,
    ca_r,
    u_s,
    u_r,
    ua_s,
    ua_r,
):
    b = lax.axis_index("batch")
    c = lax.axis_index("centers")
    n = nb * nc
    me = b * nc + c
    rows, dim = feat.shape
    cdev = cen.shape[0]
    pts = owner.shape[0]
    slots = packed.shape[1] // nc
    qb = packed.shape[2]
    piece = cdev // nb
    rows_total = rows * n

    def copy(src, dst, ssem, rsem, db, dc):
        return pltpu.make_async_remote_copy(
            src_ref=src,
            dst_ref=dst,
            send_sem=ssem,
            recv_sem=rsem,
            device_id=(db, dc),
            device_id_type=MESH,
        )

    barrier = pltpu.get_barrier_semaphore()

    @pl.loop(1, n)
    def _(k):
        d = lax.rem(me + k, n)
        pl.semaphore_signal(
            barrier, inc=1, device_id=(lax.div(d, nc), lax.rem(d, nc)), device_id_type=MESH
        )

    cval = cen[...]
    csq = cval * cval
    ncol = jnp.mean(csq, axis=1, keepdims=True) + EPS
    sb_col = jnp.sqrt(ncol)
    chat = cval / (sb_col * dim)
    wb = wts[...] * sb_col
    sb_row = jnp.sqrt(dot(jnp.full((8, dim), 1.0 / dim, jnp.float32), csq, 1, 1)[0:1] + EPS)
    a = feat[...]
    sa = jnp.sqrt(jnp.mean(a * a, axis=1, keepdims=True) + EPS)

    pl.semaphore_wait(barrier, n - 1)

    def f_copy(k):
        return copy(feat, feat_all.at[c], f_s.at[k], f_r.at[c], b, lax.rem(c + k, nc))

    @pl.loop(1, nc)
    def _(k):
        f_copy(k).start()

    own = owner[...]
    hot = (own == lax.broadcasted_iota(jnp.int32, (pts, nc), 1)).astype(jnp.float32)
    lower = (
        lax.broadcasted_iota(jnp.int32, (pts, pts), 0)
        > lax.broadcasted_iota(jnp.int32, (pts, pts), 1)
    ).astype(jnp.float32)
    rank = jnp.sum(dot(lower, hot, 1, 0) * hot, axis=1, keepdims=True).astype(jnp.int32)
    lanes = lax.broadcasted_iota(jnp.int32, (pts, nc * slots), 1)
    place = (lanes == own * slots + rank).astype(jnp.float32)
    rowsp = dot(place, eig[...], 0, 0)
    for j in range(nb):
        packed[j] = rowsp[:, j * qb : (j + 1) * qb]
    here = (lanes == c * slots + rank).astype(jnp.float32)
    marks = dot(hot * (offset[...].astype(jnp.float32) + 1.0), here, 0, 0)
    for j in range(nc):
        offsend[j] = marks[j : j + 1]

    def e_copy(k):
        d = lax.rem(me + k, n)
        db, dc = lax.div(d, nc), lax.rem(d, nc)
        return copy(
            packed.at[db, pl.ds(pl.multiple_of(dc * slots, slots), slots)],
            eigrx.at[me],
            e_s.at[k],
            e_r.at[me],
            db,
            dc,
        )

    def o_copy(k):
        d = lax.rem(me + k, n)
        db, dc = lax.div(d, nc), lax.rem(d, nc)
        return copy(offsend.at[dc], offrx.at[me], o_s.at[k], o_r.at[me], db, dc)

    @pl.loop(1, n)
    def _(k):
        o_copy(k).start()
        e_copy(k).start()

    eigrx[me] = packed[b, pl.ds(pl.multiple_of(c * slots, slots), slots)]
    offrx[me] = offsend[c]

    def block(av):
        na = jnp.mean(av * av, axis=1, keepdims=True) + EPS
        k = tangent_kernel(dot(av * lax.rsqrt(na), chat, 1, 1))
        return k, dot(k, wb, 1, 0)

    kown, pown = block(a)
    kbuf[c] = kown
    prx[c] = pown

    def p_copy(k):
        s = lax.rem(c - k + nc, nc)
        return copy(ppart.at[s], prx.at[c], p_s.at[k], p_r.at[c], b, s)

    @pl.loop(1, nc)
    def _(k):
        s = lax.rem(c - k + nc, nc)
        copy(feat, feat_all.at[s], f_s.at[k], f_r.at[s], b, s).wait_recv()
        kv, pv = block(feat_all[s])
        kbuf[s] = kv
        ppart[s] = pv
        p_copy(k).start()

    @pl.loop(1, nc)
    def _(k):
        s = lax.rem(c + k, nc)
        copy(ppart.at[s], prx.at[s], p_s.at[k], p_r.at[s], b, s).wait_recv()

    pred = prx[0]
    for j in range(1, nc):
        pred = pred + prx[j]
    resid = pred * sa - targ[...]
    rs = resid * (sa / math.sqrt(rows_total))
    rsend[...] = rs
    rrx[c] = rs

    def r_copy(k):
        return copy(rsend, rrx.at[c], r_s.at[k], r_r.at[c], b, lax.rem(c + k, nc))

    @pl.loop(1, nc)
    def _(k):
        r_copy(k).start()

    res_out[...] = resid

    @pl.loop(1, nc)
    def _(k):
        s = lax.rem(c - k + nc, nc)
        copy(rsend, rrx.at[s], r_s.at[k], r_r.at[s], b, s).wait_recv()

    outs = rsend.shape[1]
    gt = (
        dot(rrx[...].reshape(nc * rows, outs), kbuf[...].reshape(nc * rows, cdev), 0, 0) * sb_row
    )

    for j in range(nb):
        gsend[j] = gt[:, j * piece : (j + 1) * piece]

    def b_scatter(k, src, dst, ssem, rsem):
        d = lax.rem(b + k, nb)
        return copy(src.at[d], dst.at[b], ssem.at[k], rsem.at[b], d, c)

    def b_gather(k, src, dst, ssem, rsem):
        d = lax.rem(b + k, nb)
        return copy(src, dst.at[b], ssem.at[k], rsem.at[b], d, c)

    def b_wait(k, src, dst, ssem, rsem):
        d = lax.rem(b + k, nb)
        copy(src, dst.at[d], ssem.at[k], rsem.at[d], d, c).wait_recv()

    for k in range(1, nb):
        b_scatter(k, gsend, grx, g_s, g_r).start()
    grx[b] = gsend[b]

    @pl.loop(1, n)
    def _(k):
        s = lax.rem(me - k + n, n)
        copy(offsend.at[0], offrx.at[s], o_s.at[k], o_r.at[s], b, c).wait_recv()
        copy(packed.at[0, pl.ds(0, slots)], eigrx.at[s], e_s.at[k], e_r.at[s], b, c).wait_recv()

    acc = None
    for j in range(nb):
        mark = offrx[j * nc]
        for i in range(1, nc):
            mark = mark + offrx[j * nc + i]
        sel = (
            lax.broadcasted_iota(jnp.int32, (cdev, nc * slots), 0) + 1 == mark.astype(jnp.int32)
        ).astype(jnp.float32)
        part = dot(sel, eigrx[j * nc : (j + 1) * nc].reshape(nc * slots, qb), 1, 0)
        acc = part if acc is None else acc + part
    ebar[...] = acc

    for k in range(1, nb):
        b_wait(k, gown, grx, g_s, g_r)
    gsum = grx[0]
    for j in range(1, nb):
        gsum = gsum + grx[j]
    gown[...] = gsum
    gall[b] = gsum
    for k in range(1, nb):
        b_gather(k, gown, gall, ga_s, ga_r).start()
    for k in range(1, nb):
        b_wait(k, gown, gall, ga_s, ga_r)

    coeff = None
    for j in range(nb):
        part = dot(gall[j], ebar[j * piece : (j + 1) * piece], 1, 0)
        coeff = part if coeff is None else coeff + part
    og = outs // nc
    for j in range(nc):
        csend[j] = coeff[j * og : (j + 1) * og]

    def c_copy(k):
        d = lax.rem(c + k, nc)
        return copy(csend.at[d], crx.at[c], c_s.at[k], c_r.at[c], b, d)

    @pl.loop(1, nc)
    def _(k):
        c_copy(k).start()

    crx[c] = csend[c]

    @pl.loop(1, nc)
    def _(k):
        s = lax.rem(c - k + nc, nc)
        copy(csend.at[0], crx.at[s], c_s.at[k], c_r.at[s], b, s).wait_recv()

    csum = crx[0]
    for j in range(1, nc):
        csum = csum + crx[j]
    csum = csum * scale[b]
    cown[...] = csum
    call[c] = csum

    def ca_copy(k):
        return copy(cown, call.at[c], ca_s.at[k], ca_r.at[c], b, lax.rem(c + k, nc))

    @pl.loop(1, nc)
    def _(k):
        ca_copy(k).start()

    @pl.loop(1, nc)
    def _(k):
        s = lax.rem(c - k + nc, nc)
        copy(cown, call.at[s], ca_s.at[k], ca_r.at[s], b, s).wait_recv()

    scaled = jnp.concatenate([call[j] for j in range(nc)], axis=0)
    for j in range(nb):
        usend[j] = dot(scaled, ebar[j * piece : (j + 1) * piece], 1, 1)
    for k in range(1, nb):
        b_scatter(k, usend, urx, u_s, u_r).start()
    urx[b] = usend[b]
    for k in range(1, nb):
        b_wait(k, uown, urx, u_s, u_r)
    usum = urx[0]
    for j in range(1, nb):
        usum = usum + urx[j]
    usum = usum - gown[...]
    uown[...] = usum
    uall[b] = usum
    for k in range(1, nb):
        b_gather(k, uown, uall, ua_s, ua_r).start()
    for k in range(1, nb):
        b_wait(k, uown, uall, ua_s, ua_r)
    for j in range(nb):
        upd_out[j * piece : (j + 1) * piece] = uall[j].T

    @pl.loop(1, nc)
    def _(k):
        f_copy(k).wait_send()
        p_copy(k).wait_send()
        r_copy(k).wait_send()
        c_copy(k).wait_send()
        ca_copy(k).wait_send()

    @pl.loop(1, n)
    def _(k):
        e_copy(k).wait_send()
        o_copy(k).wait_send()

    for k in range(1, nb):
        b_scatter(k, gsend, grx, g_s, g_r).wait_send()
        b_gather(k, gown, gall, ga_s, ga_r).wait_send()
        b_scatter(k, usend, urx, u_s, u_r).wait_send()
        b_gather(k, uown, uall, ua_s, ua_r).wait_send()


def per_device(
    pool_features,
    pool_targets,
    batch_index,
    centers,
    weights,
    eig_vectors,
    eig_scale,
    nys_owner,
    nys_offset,
):
    nb, nc = lax.axis_size("batch"), lax.axis_size("centers")
    n = nb * nc
    feat = pool_features[batch_index]
    targ = pool_targets[batch_index]
    rows, dim = feat.shape
    outs = targ.shape[1]
    cdev = centers.shape[0]
    pts, q = eig_vectors.shape
    slots = max(2, 2 * pts // nc)
    qb, piece, og = q // nb, cdev // nb, outs // nc
    f32 = jnp.float32
    vm = pltpu.VMEM
    dma = pltpu.SemaphoreType.DMA
    spec = pl.BlockSpec(memory_space=pltpu.VMEM)
    pair = [dma((nc,)), dma((nc,))]
    every = [dma((n,)), dma((n,))]
    quad = [dma((nb,)), dma((nb,))]
    return pl.pallas_call(
        functools.partial(body, nb, nc),
        out_shape=(
            jax.ShapeDtypeStruct((rows, outs), f32),
            jax.ShapeDtypeStruct((cdev, outs), f32),
        ),
        in_specs=[spec] * 8,
        out_specs=(spec, spec),
        scratch_shapes=[
            vm((nc, rows, dim), f32),
            vm((nc, rows, cdev), f32),
            vm((nc, rows, outs), f32),
            vm((nc, rows, outs), f32),
            vm((rows, outs), f32),
            vm((nc, rows, outs), f32),
            vm((nb, nc * slots, qb), f32),
            vm((n, slots, qb), f32),
            vm((nc, 1, nc * slots), f32),
            vm((n, 1, nc * slots), f32),
            vm((cdev, qb), f32),
            vm((nb, outs, piece), f32),
            vm((nb, outs, piece), f32),
            vm((outs, piece), f32),
            vm((nb, outs, piece), f32),
            vm((nc, og, qb), f32),
            vm((nc, og, qb), f32),
            vm((og, qb), f32),
            vm((nc, og, qb), f32),
            vm((nb, outs, piece), f32),
            vm((nb, outs, piece), f32),
            vm((outs, piece), f32),
            vm((nb, outs, piece), f32),
        ]
        + pair * 3
        + every * 2
        + quad * 2
        + pair * 2
        + quad * 2,
        compiler_params=pltpu.CompilerParams(collective_id=0, has_side_effects=True),
    )(
        feat,
        targ,
        centers,
        weights,
        eig_vectors,
        eig_scale.reshape(nb, 1, qb),
        nys_owner,
        nys_offset[:, None],
    )


def solution(mesh):
    placed = (
        P(("batch", "centers"), None),
        P(("batch", "centers"), None),
        P(("batch", "centers")),
        P("centers", None),
        P("centers", None),
        P(("batch", "centers"), None),
        P(),
        P(("batch", "centers"), None),
        P(("batch", "centers")),
    )
    return jax.shard_map(
        per_device,
        mesh=mesh,
        in_specs=placed,
        out_specs=(P(("batch", "centers"), None), P("centers", None)),
        check_vma=False,
    )
```

```python
import functools
import math

import jax
import jax.numpy as jnp
from jax import lax
from jax.experimental import pallas as pl
from jax.experimental.pallas import tpu as pltpu
from jax.sharding import PartitionSpec as P

DEPTH = 3
EPS = 1e-06
HIGH = lax.Precision.HIGHEST
MESH = pl.DeviceIdType.MESH
ACOS = (
    1.5707963050,
    -0.2145988016,
    0.0889789874,
    -0.0501743046,
    0.0308918810,
    -0.0170881256,
    0.0066700901,
    -0.0012624911,
)


def dot(a, b, ca, cb):
    return lax.dot_general(
        a,
        b,
        (((ca,), (cb,)), ((), ())),
        precision=HIGH,
        preferred_element_type=jnp.float32,
    )


def arc_parts(x):
    u = jnp.maximum(1.0 - x, 1e-30)
    poly = jnp.full_like(x, ACOS[-1] / math.pi)
    for a in ACOS[-2::-1]:
        poly = poly * x + a / math.pi
    v = u * (1.0 + x)
    return u * lax.rsqrt(u) * poly, v * lax.rsqrt(v) * (1.0 / math.pi)


def tangent_kernel(cosine):
    arc, sine = arc_parts(jnp.abs(cosine))
    remain = jnp.where(cosine < 0.0, arc, 1.0 - arc)
    prod = remain * cosine
    sigma = sine + prod
    tangent = sigma + prod
    for _ in range(DEPTH - 1):
        arc, sine = arc_parts(sigma)
        remain = 1.0 - arc
        sigma = sine + remain * sigma
        tangent = sigma + tangent * remain
    return tangent


def body(
    nb,
    nc,
    pool_f,
    pool_t,
    index,
    cen,
    wts,
    eig,
    scale,
    owner,
    offset,
    res_out,
    upd_out,
    feat,
    feat_all,
    kbuf,
    ppart,
    prx,
    rsend,
    rrx,
    packed,
    eigrx,
    offsend,
    offrx,
    ebar,
    gsend,
    grx,
    gown,
    gall,
    csend,
    crx,
    cown,
    call,
    usend,
    urx,
    uown,
    uall,
    f_s,
    f_r,
    p_s,
    p_r,
    r_s,
    r_r,
    e_s,
    e_r,
    o_s,
    o_r,
    g_s,
    g_r,
    ga_s,
    ga_r,
    c_s,
    c_r,
    ca_s,
    ca_r,
    u_s,
    u_r,
    ua_s,
    ua_r,
):
    b = lax.axis_index("batch")
    c = lax.axis_index("centers")
    n = nb * nc
    me = b * nc + c
    rows, dim = feat.shape
    cdev = cen.shape[0]
    pts = owner.shape[1]
    slots = packed.shape[1] // nc
    qb = packed.shape[2]
    piece = cdev // nb
    rows_total = rows * n

    def copy(src, dst, ssem, rsem, db, dc):
        return pltpu.make_async_remote_copy(
            src_ref=src,
            dst_ref=dst,
            send_sem=ssem,
            recv_sem=rsem,
            device_id=(db, dc),
            device_id_type=MESH,
        )

    barrier = pltpu.get_barrier_semaphore()

    @pl.loop(1, n)
    def _(k):
        d = lax.rem(me + k, n)
        pl.semaphore_signal(
            barrier, inc=1, device_id=(lax.div(d, nc), lax.rem(d, nc)), device_id_type=MESH
        )

    drawn = (
        lax.broadcasted_iota(jnp.int32, (pool_f.shape[0], rows), 0) == index[...]
    ).astype(jnp.float32)
    feat[...] = dot(drawn, pool_f[...], 0, 0)
    cval = cen[...]
    csq = cval * cval
    ncol = jnp.mean(csq, axis=1, keepdims=True) + EPS
    sb_col = jnp.sqrt(ncol)
    chat = cval / (sb_col * dim)
    sb_row = jnp.sqrt(dot(jnp.full((8, dim), 1.0 / dim, jnp.float32), csq, 1, 1)[0:1] + EPS)
    wb = wts[...] * sb_row
    a = feat[...]
    sa = jnp.sqrt(jnp.mean(a * a, axis=1, keepdims=True) + EPS)

    pl.semaphore_wait(barrier, n - 1)

    def f_copy(k):
        return copy(feat, feat_all.at[c], f_s.at[k], f_r.at[c], b, lax.rem(c + k, nc))

    @pl.loop(1, nc)
    def _(k):
        f_copy(k).start()

    own = owner[...]
    hot = (own == lax.broadcasted_iota(jnp.int32, (nc, pts), 0)).astype(jnp.float32)
    upper = (
        lax.broadcasted_iota(jnp.int32, (pts, pts), 0)
        < lax.broadcasted_iota(jnp.int32, (pts, pts), 1)
    ).astype(jnp.float32)
    rank = jnp.sum(dot(hot, upper, 1, 0) * hot, axis=0, keepdims=True).astype(jnp.int32)
    spots = lax.broadcasted_iota(jnp.int32, (nc * slots, pts), 0)
    place = (spots == own * slots + rank).astype(jnp.float32)
    rowsp = dot(place, eig[...], 1, 0)
    for j in range(nb):
        packed[j] = rowsp[:, j * qb : (j + 1) * qb]
    here = (spots == c * slots + rank).astype(jnp.float32)
    marks = dot(hot * (offset[...].astype(jnp.float32) + 1.0), here, 1, 1)
    for j in range(nc):
        offsend[j] = marks[j : j + 1]

    def e_copy(k):
        d = lax.rem(me + k, n)
        db, dc = lax.div(d, nc), lax.rem(d, nc)
        return copy(
            packed.at[db, pl.ds(pl.multiple_of(dc * slots, slots), slots)],
            eigrx.at[me],
            e_s.at[k],
            e_r.at[me],
            db,
            dc,
        )

    def o_copy(k):
        d = lax.rem(me + k, n)
        db, dc = lax.div(d, nc), lax.rem(d, nc)
        return copy(offsend.at[dc], offrx.at[me], o_s.at[k], o_r.at[me], db, dc)

    @pl.loop(1, n)
    def _(k):
        o_copy(k).start()
        e_copy(k).start()

    eigrx[me] = packed[b, pl.ds(pl.multiple_of(c * slots, slots), slots)]
    offrx[me] = offsend[c]

    targ = dot(pool_t[...], drawn, 1, 0).T

    def block(av):
        na = jnp.mean(av * av, axis=1, keepdims=True) + EPS
        k = tangent_kernel(dot(av * lax.rsqrt(na), chat, 1, 1))
        return k, dot(k, wb, 1, 1)

    kown, pown = block(a)
    kbuf[c] = kown
    prx[c] = pown

    def p_copy(k):
        s = lax.rem(c - k + nc, nc)
        return copy(ppart.at[s], prx.at[c], p_s.at[k], p_r.at[c], b, s)

    @pl.loop(1, nc)
    def _(k):
        s = lax.rem(c - k + nc, nc)
        copy(feat, feat_all.at[s], f_s.at[k], f_r.at[s], b, s).wait_recv()
        kv, pv = block(feat_all[s])
        kbuf[s] = kv
        ppart[s] = pv
        p_copy(k).start()

    @pl.loop(1, nc)
    def _(k):
        s = lax.rem(c + k, nc)
        copy(ppart.at[s], prx.at[s], p_s.at[k], p_r.at[s], b, s).wait_recv()

    pred = prx[0]
    for j in range(1, nc):
        pred = pred + prx[j]
    resid = pred * sa - targ
    rs = resid * (sa / math.sqrt(rows_total))
    rsend[...] = rs
    rrx[c] = rs

    def r_copy(k):
        return copy(rsend, rrx.at[c], r_s.at[k], r_r.at[c], b, lax.rem(c + k, nc))

    @pl.loop(1, nc)
    def _(k):
        r_copy(k).start()

    res_out[...] = resid

    @pl.loop(1, nc)
    def _(k):
        s = lax.rem(c - k + nc, nc)
        copy(rsend, rrx.at[s], r_s.at[k], r_r.at[s], b, s).wait_recv()

    outs = rsend.shape[1]
    gt = (
        dot(rrx[...].reshape(nc * rows, outs), kbuf[...].reshape(nc * rows, cdev), 0, 0) * sb_row
    )

    for j in range(nb):
        gsend[j] = gt[:, j * piece : (j + 1) * piece]

    def b_scatter(k, src, dst, ssem, rsem):
        d = lax.rem(b + k, nb)
        return copy(src.at[d], dst.at[b], ssem.at[k], rsem.at[b], d, c)

    def b_gather(k, src, dst, ssem, rsem):
        d = lax.rem(b + k, nb)
        return copy(src, dst.at[b], ssem.at[k], rsem.at[b], d, c)

    def b_wait(k, src, dst, ssem, rsem):
        d = lax.rem(b + k, nb)
        copy(src, dst.at[d], ssem.at[k], rsem.at[d], d, c).wait_recv()

    for k in range(1, nb):
        b_scatter(k, gsend, grx, g_s, g_r).start()
    grx[b] = gsend[b]

    @pl.loop(1, n)
    def _(k):
        s = lax.rem(me - k + n, n)
        copy(offsend.at[0], offrx.at[s], o_s.at[k], o_r.at[s], b, c).wait_recv()
        copy(packed.at[0, pl.ds(0, slots)], eigrx.at[s], e_s.at[k], e_r.at[s], b, c).wait_recv()

    acc = None
    for j in range(nb):
        mark = offrx[j * nc]
        for i in range(1, nc):
            mark = mark + offrx[j * nc + i]
        sel = (
            lax.broadcasted_iota(jnp.int32, (cdev, nc * slots), 0) + 1 == mark.astype(jnp.int32)
        ).astype(jnp.float32)
        part = dot(sel, eigrx[j * nc : (j + 1) * nc].reshape(nc * slots, qb), 1, 0)
        acc = part if acc is None else acc + part
    ebar[...] = acc

    for k in range(1, nb):
        b_wait(k, gown, grx, g_s, g_r)
    gsum = grx[0]
    for j in range(1, nb):
        gsum = gsum + grx[j]
    gown[...] = gsum
    gall[b] = gsum
    for k in range(1, nb):
        b_gather(k, gown, gall, ga_s, ga_r).start()
    for k in range(1, nb):
        b_wait(k, gown, gall, ga_s, ga_r)

    coeff = None
    for j in range(nb):
        part = dot(gall[j], ebar[j * piece : (j + 1) * piece], 1, 0)
        coeff = part if coeff is None else coeff + part
    og = outs // nc
    for j in range(nc):
        csend[j] = coeff[j * og : (j + 1) * og]

    def c_copy(k):
        d = lax.rem(c + k, nc)
        return copy(csend.at[d], crx.at[c], c_s.at[k], c_r.at[c], b, d)

    @pl.loop(1, nc)
    def _(k):
        c_copy(k).start()

    crx[c] = csend[c]

    @pl.loop(1, nc)
    def _(k):
        s = lax.rem(c - k + nc, nc)
        copy(csend.at[0], crx.at[s], c_s.at[k], c_r.at[s], b, s).wait_recv()

    csum = crx[0]
    for j in range(1, nc):
        csum = csum + crx[j]
    csum = csum * scale[b]
    cown[...] = csum
    call[c] = csum

    def ca_copy(k):
        return copy(cown, call.at[c], ca_s.at[k], ca_r.at[c], b, lax.rem(c + k, nc))

    @pl.loop(1, nc)
    def _(k):
        ca_copy(k).start()

    @pl.loop(1, nc)
    def _(k):
        s = lax.rem(c - k + nc, nc)
        copy(cown, call.at[s], ca_s.at[k], ca_r.at[s], b, s).wait_recv()

    scaled = jnp.concatenate([call[j] for j in range(nc)], axis=0)
    for j in range(nb):
        usend[j] = dot(scaled, ebar[j * piece : (j + 1) * piece], 1, 1)
    for k in range(1, nb):
        b_scatter(k, usend, urx, u_s, u_r).start()
    urx[b] = usend[b]
    for k in range(1, nb):
        b_wait(k, uown, urx, u_s, u_r)
    usum = urx[0]
    for j in range(1, nb):
        usum = usum + urx[j]
    usum = usum - gown[...]
    uown[...] = usum
    uall[b] = usum
    for k in range(1, nb):
        b_gather(k, uown, uall, ua_s, ua_r).start()
    for k in range(1, nb):
        b_wait(k, uown, uall, ua_s, ua_r)
    for j in range(nb):
        upd_out[:, j * piece : (j + 1) * piece] = uall[j]

    @pl.loop(1, nc)
    def _(k):
        f_copy(k).wait_send()
        p_copy(k).wait_send()
        r_copy(k).wait_send()
        c_copy(k).wait_send()
        ca_copy(k).wait_send()

    @pl.loop(1, n)
    def _(k):
        e_copy(k).wait_send()
        o_copy(k).wait_send()

    for k in range(1, nb):
        b_scatter(k, gsend, grx, g_s, g_r).wait_send()
        b_gather(k, gown, gall, ga_s, ga_r).wait_send()
        b_scatter(k, usend, urx, u_s, u_r).wait_send()
        b_gather(k, uown, uall, ua_s, ua_r).wait_send()


def per_device(
    pool_features,
    pool_targets,
    batch_index,
    centers,
    weights,
    eig_vectors,
    eig_scale,
    nys_owner,
    nys_offset,
):
    nb, nc = lax.axis_size("batch"), lax.axis_size("centers")
    n = nb * nc
    rows, dim = batch_index.shape[0], pool_features.shape[1]
    outs = pool_targets.shape[1]
    cdev = centers.shape[0]
    pts, q = eig_vectors.shape
    slots = max(2, 2 * pts // nc)
    qb, piece, og = q // nb, cdev // nb, outs // nc
    f32 = jnp.float32
    vm = pltpu.VMEM
    dma = pltpu.SemaphoreType.DMA
    spec = pl.BlockSpec(memory_space=pltpu.VMEM)
    pair = [dma((nc,)), dma((nc,))]
    every = [dma((n,)), dma((n,))]
    quad = [dma((nb,)), dma((nb,))]
    residual, update = pl.pallas_call(
        functools.partial(body, nb, nc),
        out_shape=(
            jax.ShapeDtypeStruct((rows, outs), f32),
            jax.ShapeDtypeStruct((outs, cdev), f32),
        ),
        in_specs=[spec] * 9,
        out_specs=(spec, spec),
        scratch_shapes=[
            vm((rows, dim), f32),
            vm((nc, rows, dim), f32),
            vm((nc, rows, cdev), f32),
            vm((nc, rows, outs), f32),
            vm((nc, rows, outs), f32),
            vm((rows, outs), f32),
            vm((nc, rows, outs), f32),
            vm((nb, nc * slots, qb), f32),
            vm((n, slots, qb), f32),
            vm((nc, 1, nc * slots), f32),
            vm((n, 1, nc * slots), f32),
            vm((cdev, qb), f32),
            vm((nb, outs, piece), f32),
            vm((nb, outs, piece), f32),
            vm((outs, piece), f32),
            vm((nb, outs, piece), f32),
            vm((nc, og, qb), f32),
            vm((nc, og, qb), f32),
            vm((og, qb), f32),
            vm((nc, og, qb), f32),
            vm((nb, outs, piece), f32),
            vm((nb, outs, piece), f32),
            vm((outs, piece), f32),
            vm((nb, outs, piece), f32),
        ]
        + pair * 3
        + every * 2
        + quad * 2
        + pair * 2
        + quad * 2,
        compiler_params=pltpu.CompilerParams(collective_id=0, has_side_effects=True),
    )(
        pool_features,
        pool_targets.T,
        batch_index[None, :],
        centers,
        weights.T,
        eig_vectors,
        eig_scale.reshape(nb, 1, qb),
        nys_owner.reshape(1, pts),
        nys_offset[None, :],
    )
    return (residual, update.T)


def solution(mesh):
    placed = (
        P(("batch", "centers"), None),
        P(("batch", "centers"), None),
        P(("batch", "centers")),
        P("centers", None),
        P("centers", None),
        P(("batch", "centers"), None),
        P(),
        P(("batch", "centers"), None),
        P(("batch", "centers")),
    )
    return jax.shard_map(
        per_device,
        mesh=mesh,
        in_specs=placed,
        out_specs=(P(("batch", "centers"), None), P("centers", None)),
        check_vma=False,
    )
```

```python
import functools
import math

import jax
import jax.numpy as jnp
from jax import lax
from jax.experimental import pallas as pl
from jax.experimental.pallas import tpu as pltpu
from jax.sharding import PartitionSpec as P

DEPTH = 3
EPS = 1e-06
HIGH = lax.Precision.HIGHEST
MESH = pl.DeviceIdType.MESH
FIRST, EACH, EARLY = 8, 14, 1
ACOS = (
    1.5707963050,
    -0.2145988016,
    0.0889789874,
    -0.0501743046,
    0.0308918810,
    -0.0170881256,
    0.0066700901,
    -0.0012624911,
)


def dot(a, b, ca, cb):
    return lax.dot_general(
        a,
        b,
        (((ca,), (cb,)), ((), ())),
        precision=HIGH,
        preferred_element_type=jnp.float32,
    )


def arc_parts(x):
    u = jnp.maximum(1.0 - x, 1e-30)
    poly = jnp.full_like(x, ACOS[-1] / math.pi)
    for a in ACOS[-2::-1]:
        poly = poly * x + a / math.pi
    v = u * (1.0 + x)
    return u * lax.rsqrt(u) * poly, v * lax.rsqrt(v) * (1.0 / math.pi)


def tangent_kernel(cosine):
    arc, sine = arc_parts(jnp.abs(cosine))
    remain = jnp.where(cosine < 0.0, arc, 1.0 - arc)
    prod = remain * cosine
    sigma = sine + prod
    tangent = sigma + prod
    for _ in range(DEPTH - 1):
        arc, sine = arc_parts(sigma)
        remain = 1.0 - arc
        sigma = sine + remain * sigma
        tangent = sigma + tangent * remain
    return tangent


def body(
    nb,
    nc,
    pool_f,
    pool_t,
    index,
    cen,
    wts,
    eig,
    scale,
    owner,
    offset,
    res_out,
    upd_out,
    feat,
    feat_all,
    kbuf,
    ppart,
    prx,
    rsend,
    rrx,
    packed,
    eigrx,
    offsend,
    offrx,
    ebar,
    gsend,
    grx,
    gown,
    gall,
    csend,
    crx,
    cown,
    call,
    usend,
    urx,
    uown,
    uall,
    f_s,
    f_r,
    p_s,
    p_r,
    r_s,
    r_r,
    e_s,
    e_r,
    o_s,
    o_r,
    g_s,
    g_r,
    ga_s,
    ga_r,
    c_s,
    c_r,
    ca_s,
    ca_r,
    u_s,
    u_r,
    ua_s,
    ua_r,
):
    b = lax.axis_index("batch")
    c = lax.axis_index("centers")
    n = nb * nc
    me = b * nc + c
    rows, dim = feat.shape
    cdev = cen.shape[0]
    pts = owner.shape[1]
    slots = packed.shape[1] // nc
    qb = packed.shape[2]
    piece = cdev // nb
    rows_total = rows * n

    def copy(src, dst, ssem, rsem, db, dc):
        return pltpu.make_async_remote_copy(
            src_ref=src,
            dst_ref=dst,
            send_sem=ssem,
            recv_sem=rsem,
            device_id=(db, dc),
            device_id_type=MESH,
        )

    barrier = pltpu.get_barrier_semaphore()

    @pl.loop(1, n)
    def _(k):
        d = lax.rem(me + k, n)
        pl.semaphore_signal(
            barrier, inc=1, device_id=(lax.div(d, nc), lax.rem(d, nc)), device_id_type=MESH
        )

    drawn = (
        lax.broadcasted_iota(jnp.int32, (pool_f.shape[0], rows), 0) == index[...]
    ).astype(jnp.float32)
    feat[...] = dot(drawn, pool_f[...], 0, 0)
    cval = cen[...]
    csq = cval * cval
    ncol = jnp.mean(csq, axis=1, keepdims=True) + EPS
    sb_col = jnp.sqrt(ncol)
    chat = cval / (sb_col * dim)
    sb_row = jnp.sqrt(dot(jnp.full((8, dim), 1.0 / dim, jnp.float32), csq, 1, 1)[0:1] + EPS)
    wb = wts[...] * sb_row
    a = feat[...]
    sa = jnp.sqrt(jnp.mean(a * a, axis=1, keepdims=True) + EPS)

    own = owner[...]
    hot = (own == lax.broadcasted_iota(jnp.int32, (nc, pts), 0)).astype(jnp.float32)
    upper = (
        lax.broadcasted_iota(jnp.int32, (pts, pts), 0)
        < lax.broadcasted_iota(jnp.int32, (pts, pts), 1)
    ).astype(jnp.float32)
    rank = jnp.sum(dot(hot, upper, 1, 0) * hot, axis=0, keepdims=True).astype(jnp.int32)
    spots = lax.broadcasted_iota(jnp.int32, (nc * slots, pts), 0)
    place = (spots == own * slots + rank).astype(jnp.float32)
    rowsp = dot(place, eig[...], 1, 0)
    for j in range(nb):
        packed[j] = rowsp[:, j * qb : (j + 1) * qb]
    here = (spots == c * slots + rank).astype(jnp.float32)
    marks = dot(hot * (offset[...].astype(jnp.float32) + 1.0), here, 1, 1)
    for j in range(nc):
        offsend[j] = marks[j : j + 1]

    eigrx[me] = packed[b, pl.ds(pl.multiple_of(c * slots, slots), slots)]
    offrx[me] = offsend[c]

    targ = dot(pool_t[...], drawn, 1, 0).T

    def block(av):
        na = jnp.mean(av * av, axis=1, keepdims=True) + EPS
        k = tangent_kernel(dot(av * lax.rsqrt(na), chat, 1, 1))
        return k, dot(k, wb, 1, 1)

    kown, pown = block(a)
    kbuf[c] = kown
    prx[c] = pown

    pl.semaphore_wait(barrier, n - 1)

    def f_copy(k):
        return copy(feat, feat_all.at[c], f_s.at[k], f_r.at[c], b, lax.rem(c + k, nc))

    @pl.loop(1, nc)
    def _(k):
        f_copy(k).start()

    def e_copy(t):
        db, dc = lax.rem(b + lax.div(t, nc), nb), lax.rem(c + lax.rem(t, nc), nc)
        return copy(
            packed.at[db, pl.ds(pl.multiple_of(dc * slots, slots), slots)],
            eigrx.at[me],
            e_s.at[t],
            e_r.at[me],
            db,
            dc,
        )

    def o_copy(t):
        db, dc = lax.rem(b + lax.div(t, nc), nb), lax.rem(c + lax.rem(t, nc), nc)
        return copy(offsend.at[dc], offrx.at[me], o_s.at[t], o_r.at[me], db, dc)

    first = (n - 1) * FIRST // 32
    each = (n - 1) * EACH // (32 * (nc - 1))
    last = first + each * (nc - 1)

    @pl.loop(1, 1 + first)
    def _(t):
        e_copy(t).start()

    def p_copy(k):
        s = lax.rem(c - k + nc, nc)
        return copy(ppart.at[s], prx.at[c], p_s.at[k], p_r.at[c], b, s)

    @pl.loop(1, nc)
    def _(k):
        s = lax.rem(c - k + nc, nc)
        copy(feat, feat_all.at[s], f_s.at[k], f_r.at[s], b, s).wait_recv()
        kv, pv = block(feat_all[s])
        kbuf[s] = kv
        ppart[s] = pv
        p_copy(k).start()

        @pl.loop(0, each)
        def _(t):
            e_copy(1 + first + (k - 1) * each + t).start()

    @pl.loop(1, nc)
    def _(k):
        s = lax.rem(c + k, nc)
        copy(ppart.at[s], prx.at[s], p_s.at[k], p_r.at[s], b, s).wait_recv()

    pred = prx[0]
    for j in range(1, nc):
        pred = pred + prx[j]
    resid = pred * sa - targ
    rs = resid * (sa / math.sqrt(rows_total))
    rsend[...] = rs
    rrx[c] = rs

    def r_copy(k):
        return copy(rsend, rrx.at[c], r_s.at[k], r_r.at[c], b, lax.rem(c + k, nc))

    @pl.loop(1, nc)
    def _(k):
        r_copy(k).start()

    @pl.loop(1, n)
    def _(t):
        o_copy(t).start()

    @pl.loop(1 + last, n)
    def _(t):
        e_copy(t).start()

    res_out[...] = resid

    @pl.loop(1, nc)
    def _(k):
        s = lax.rem(c - k + nc, nc)
        copy(rsend, rrx.at[s], r_s.at[k], r_r.at[s], b, s).wait_recv()

    outs = rsend.shape[1]
    gt = (
        dot(rrx[...].reshape(nc * rows, outs), kbuf[...].reshape(nc * rows, cdev), 0, 0) * sb_row
    )

    for j in range(nb):
        gsend[j] = gt[:, j * piece : (j + 1) * piece]

    def b_scatter(k, src, dst, ssem, rsem):
        d = lax.rem(b + k, nb)
        return copy(src.at[d], dst.at[b], ssem.at[k], rsem.at[b], d, c)

    def b_gather(k, src, dst, ssem, rsem):
        d = lax.rem(b + k, nb)
        return copy(src, dst.at[b], ssem.at[k], rsem.at[b], d, c)

    def b_wait(k, src, dst, ssem, rsem):
        d = lax.rem(b + k, nb)
        copy(src, dst.at[d], ssem.at[k], rsem.at[d], d, c).wait_recv()

    for k in range(1, nb):
        b_scatter(k, gsend, grx, g_s, g_r).start()
    grx[b] = gsend[b]

    def add_group(j):
        g = lax.rem(b - j + nb, nb) * nc

        @pl.loop(1 if j == 0 else 0, nc)
        def _(i):
            s = g + lax.rem(c - i + nc, nc)
            copy(offsend.at[0], offrx.at[s], o_s.at[i], o_r.at[s], b, c).wait_recv()
            copy(packed.at[0, pl.ds(0, slots)], eigrx.at[s], e_s.at[i], e_r.at[s], b, c).wait_recv()

        mark = offrx[g]
        for i in range(1, nc):
            mark = mark + offrx[g + i]
        sel = (
            lax.broadcasted_iota(jnp.int32, (cdev, nc * slots), 0) + 1 == mark.astype(jnp.int32)
        ).astype(jnp.float32)
        part = dot(sel, eigrx[pl.ds(g, nc)].reshape(nc * slots, qb), 1, 0)
        ebar[...] = part if j == 0 else ebar[...] + part

    early = min(EARLY, nb)
    for j in range(early):
        add_group(j)

    for k in range(1, nb):
        b_wait(k, gown, grx, g_s, g_r)
    gsum = grx[0]
    for j in range(1, nb):
        gsum = gsum + grx[j]
    gown[...] = gsum
    gall[b] = gsum
    for k in range(1, nb):
        b_gather(k, gown, gall, ga_s, ga_r).start()
    for j in range(early, nb):
        add_group(j)
    for k in range(1, nb):
        b_wait(k, gown, gall, ga_s, ga_r)

    coeff = None
    for j in range(nb):
        part = dot(gall[j], ebar[j * piece : (j + 1) * piece], 1, 0)
        coeff = part if coeff is None else coeff + part
    og = outs // nc
    for j in range(nc):
        csend[j] = coeff[j * og : (j + 1) * og]

    def c_copy(k):
        d = lax.rem(c + k, nc)
        return copy(csend.at[d], crx.at[c], c_s.at[k], c_r.at[c], b, d)

    @pl.loop(1, nc)
    def _(k):
        c_copy(k).start()

    crx[c] = csend[c]

    @pl.loop(1, nc)
    def _(k):
        s = lax.rem(c - k + nc, nc)
        copy(csend.at[0], crx.at[s], c_s.at[k], c_r.at[s], b, s).wait_recv()

    csum = crx[0]
    for j in range(1, nc):
        csum = csum + crx[j]
    csum = csum * scale[b]
    cown[...] = csum
    call[c] = csum

    def ca_copy(k):
        return copy(cown, call.at[c], ca_s.at[k], ca_r.at[c], b, lax.rem(c + k, nc))

    @pl.loop(1, nc)
    def _(k):
        ca_copy(k).start()

    @pl.loop(1, nc)
    def _(k):
        s = lax.rem(c - k + nc, nc)
        copy(cown, call.at[s], ca_s.at[k], ca_r.at[s], b, s).wait_recv()

    scaled = jnp.concatenate([call[j] for j in range(nc)], axis=0)
    for j in range(nb):
        usend[j] = dot(scaled, ebar[j * piece : (j + 1) * piece], 1, 1)
    for k in range(1, nb):
        b_scatter(k, usend, urx, u_s, u_r).start()
    urx[b] = usend[b]
    for k in range(1, nb):
        b_wait(k, uown, urx, u_s, u_r)
    usum = urx[0]
    for j in range(1, nb):
        usum = usum + urx[j]
    usum = usum - gown[...]
    uown[...] = usum
    uall[b] = usum
    for k in range(1, nb):
        b_gather(k, uown, uall, ua_s, ua_r).start()
    for k in range(1, nb):
        b_wait(k, uown, uall, ua_s, ua_r)
    for j in range(nb):
        upd_out[:, j * piece : (j + 1) * piece] = uall[j]

    @pl.loop(1, nc)
    def _(k):
        f_copy(k).wait_send()
        p_copy(k).wait_send()
        r_copy(k).wait_send()
        c_copy(k).wait_send()
        ca_copy(k).wait_send()

    @pl.loop(1, n)
    def _(k):
        e_copy(k).wait_send()
        o_copy(k).wait_send()

    for k in range(1, nb):
        b_scatter(k, gsend, grx, g_s, g_r).wait_send()
        b_gather(k, gown, gall, ga_s, ga_r).wait_send()
        b_scatter(k, usend, urx, u_s, u_r).wait_send()
        b_gather(k, uown, uall, ua_s, ua_r).wait_send()


def per_device(
    pool_features,
    pool_targets,
    batch_index,
    centers,
    weights,
    eig_vectors,
    eig_scale,
    nys_owner,
    nys_offset,
):
    nb, nc = lax.axis_size("batch"), lax.axis_size("centers")
    n = nb * nc
    rows, dim = batch_index.shape[0], pool_features.shape[1]
    outs = pool_targets.shape[1]
    cdev = centers.shape[0]
    pts, q = eig_vectors.shape
    slots = max(2, 2 * pts // nc)
    qb, piece, og = q // nb, cdev // nb, outs // nc
    f32 = jnp.float32
    vm = pltpu.VMEM
    dma = pltpu.SemaphoreType.DMA
    spec = pl.BlockSpec(memory_space=pltpu.VMEM)
    pair = [dma((nc,)), dma((nc,))]
    every = [dma((n,)), dma((n,))]
    quad = [dma((nb,)), dma((nb,))]
    residual, update = pl.pallas_call(
        functools.partial(body, nb, nc),
        out_shape=(
            jax.ShapeDtypeStruct((rows, outs), f32),
            jax.ShapeDtypeStruct((outs, cdev), f32),
        ),
        in_specs=[spec] * 9,
        out_specs=(spec, spec),
        scratch_shapes=[
            vm((rows, dim), f32),
            vm((nc, rows, dim), f32),
            vm((nc, rows, cdev), f32),
            vm((nc, rows, outs), f32),
            vm((nc, rows, outs), f32),
            vm((rows, outs), f32),
            vm((nc, rows, outs), f32),
            vm((nb, nc * slots, qb), f32),
            vm((n, slots, qb), f32),
            vm((nc, 1, nc * slots), f32),
            vm((n, 1, nc * slots), f32),
            vm((cdev, qb), f32),
            vm((nb, outs, piece), f32),
            vm((nb, outs, piece), f32),
            vm((outs, piece), f32),
            vm((nb, outs, piece), f32),
            vm((nc, og, qb), f32),
            vm((nc, og, qb), f32),
            vm((og, qb), f32),
            vm((nc, og, qb), f32),
            vm((nb, outs, piece), f32),
            vm((nb, outs, piece), f32),
            vm((outs, piece), f32),
            vm((nb, outs, piece), f32),
        ]
        + pair * 3
        + every * 2
        + quad * 2
        + pair * 2
        + quad * 2,
        compiler_params=pltpu.CompilerParams(collective_id=0, has_side_effects=True),
    )(
        pool_features,
        pool_targets.T,
        batch_index[None, :],
        centers,
        weights.T,
        eig_vectors,
        eig_scale.reshape(nb, 1, qb),
        nys_owner.reshape(1, pts),
        nys_offset[None, :],
    )
    return (residual, update.T)


def solution(mesh):
    placed = (
        P(("batch", "centers"), None),
        P(("batch", "centers"), None),
        P(("batch", "centers")),
        P("centers", None),
        P("centers", None),
        P(("batch", "centers"), None),
        P(),
        P(("batch", "centers"), None),
        P(("batch", "centers")),
    )
    return jax.shard_map(
        per_device,
        mesh=mesh,
        in_specs=placed,
        out_specs=(P(("batch", "centers"), None), P("centers", None)),
        check_vma=False,
    )
```

```python
import functools
import math

import jax
import jax.numpy as jnp
from jax import lax
from jax.experimental import pallas as pl
from jax.experimental.pallas import tpu as pltpu
from jax.sharding import PartitionSpec as P

DEPTH = 3
EPS = 1e-06
HIGH = lax.Precision.HIGHEST
MESH = pl.DeviceIdType.MESH
FIRST, EACH, EARLY = 16, 0, 1
ACOS = (
    1.5707963050,
    -0.2145988016,
    0.0889789874,
    -0.0501743046,
    0.0308918810,
    -0.0170881256,
    0.0066700901,
    -0.0012624911,
)


def dot(a, b, ca, cb):
    return lax.dot_general(
        a,
        b,
        (((ca,), (cb,)), ((), ())),
        precision=HIGH,
        preferred_element_type=jnp.float32,
    )


def pick(onehot, x):
    low = jnp.bfloat16
    hi = x.astype(low)
    rest = x - hi.astype(jnp.float32)
    mid = rest.astype(low)
    parts = (rest - mid.astype(jnp.float32)).astype(low), mid, hi
    total = None
    for p in parts:
        part = jnp.dot(onehot, p, preferred_element_type=jnp.float32)
        total = part if total is None else total + part
    return total


def fold(x):
    h = x.shape[0] // 2
    return jnp.concatenate([x[:h], x[h:]], axis=1)


def unfold(x):
    h = x.shape[1] // 2
    return jnp.concatenate([x[:, :h], x[:, h:]], axis=0)


def arc_parts(x):
    u = jnp.maximum(1.0 - x, 1e-30)
    poly = jnp.full_like(x, ACOS[-1] / math.pi)
    for a in ACOS[-2::-1]:
        poly = poly * x + a / math.pi
    v = u * (1.0 + x)
    return u * lax.rsqrt(u) * poly, v * lax.rsqrt(v) * (1.0 / math.pi)


def tangent_kernel(cosine):
    arc, sine = arc_parts(jnp.abs(cosine))
    remain = jnp.where(cosine < 0.0, arc, 1.0 - arc)
    prod = remain * cosine
    sigma = sine + prod
    tangent = sigma + prod
    for _ in range(DEPTH - 1):
        arc, sine = arc_parts(sigma)
        remain = 1.0 - arc
        sigma = sine + remain * sigma
        tangent = sigma + tangent * remain
    return tangent


def body(
    nb,
    nc,
    pool_f,
    pool_t,
    index,
    cen,
    wts,
    eig,
    scale,
    owner,
    offset,
    res_out,
    upd_out,
    feat,
    feat_all,
    kbuf,
    ppart,
    prx,
    rsend,
    rrx,
    packed,
    eigrx,
    offsend,
    offrx,
    ebar,
    gsend,
    grx,
    gown,
    gall,
    csend,
    crx,
    cown,
    call,
    usend,
    urx,
    uown,
    uall,
    f_s,
    f_r,
    p_s,
    p_r,
    r_s,
    r_r,
    e_s,
    e_r,
    o_s,
    o_r,
    g_s,
    g_r,
    ga_s,
    ga_r,
    c_s,
    c_r,
    ca_s,
    ca_r,
    u_s,
    u_r,
    ua_s,
    ua_r,
):
    b = lax.axis_index("batch")
    c = lax.axis_index("centers")
    n = nb * nc
    me = b * nc + c
    rows, dim = feat.shape
    cdev = cen.shape[0]
    pts = owner.shape[1]
    slots = packed.shape[1] // nc
    qb = packed.shape[2]
    piece = cdev // nb
    rows_total = rows * n

    def copy(src, dst, ssem, rsem, db, dc):
        return pltpu.make_async_remote_copy(
            src_ref=src,
            dst_ref=dst,
            send_sem=ssem,
            recv_sem=rsem,
            device_id=(db, dc),
            device_id_type=MESH,
        )

    barrier = pltpu.get_barrier_semaphore()

    @pl.loop(1, n)
    def _(k):
        d = lax.rem(me + k, n)
        pl.semaphore_signal(
            barrier, inc=1, device_id=(lax.div(d, nc), lax.rem(d, nc)), device_id_type=MESH
        )

    drawn = (
        lax.broadcasted_iota(jnp.int32, (pool_f.shape[0], rows), 0) == index[...]
    ).astype(jnp.float32)
    feat[...] = dot(drawn, pool_f[...], 0, 0)
    cval = cen[...]
    csq = cval * cval
    ncol = jnp.mean(csq, axis=1, keepdims=True) + EPS
    sb_col = jnp.sqrt(ncol)
    chat = cval / (sb_col * dim)
    sb_row = jnp.sqrt(dot(jnp.full((8, dim), 1.0 / dim, jnp.float32), csq, 1, 1)[0:1] + EPS)
    wb = wts[...] * sb_row
    a = feat[...]
    sa = jnp.sqrt(jnp.mean(a * a, axis=1, keepdims=True) + EPS)

    own = owner[...]
    hot = (own == lax.broadcasted_iota(jnp.int32, (nc, pts), 0)).astype(jnp.float32)
    upper = (
        lax.broadcasted_iota(jnp.int32, (pts, pts), 0)
        < lax.broadcasted_iota(jnp.int32, (pts, pts), 1)
    ).astype(jnp.float32)
    rank = jnp.sum(dot(hot, upper, 1, 0) * hot, axis=0, keepdims=True).astype(jnp.int32)
    spots = lax.broadcasted_iota(jnp.int32, (nc * slots, pts), 0)
    place = (spots == own * slots + rank).astype(jnp.float32)
    rowsp = dot(place, eig[...], 1, 0)
    for j in range(nb):
        packed[j] = rowsp[:, j * qb : (j + 1) * qb]
    here = (spots == c * slots + rank).astype(jnp.float32)
    marks = dot(hot * (offset[...].astype(jnp.float32) + 1.0), here, 1, 1)
    for j in range(nc):
        offsend[j] = marks[j : j + 1]

    eigrx[me] = packed[b, pl.ds(pl.multiple_of(c * slots, slots), slots)]
    offrx[me] = offsend[c]

    targ = dot(pool_t[...], drawn, 1, 0).T

    def block(av):
        na = jnp.mean(av * av, axis=1, keepdims=True) + EPS
        k = tangent_kernel(dot(av * lax.rsqrt(na), chat, 1, 1))
        return k, fold(dot(k, wb, 1, 1))

    kown, pown = block(a)
    kbuf[c] = kown
    prx[c] = pown

    pl.semaphore_wait(barrier, n - 1)

    def f_copy(k):
        return copy(feat, feat_all.at[c], f_s.at[k], f_r.at[c], b, lax.rem(c + k, nc))

    @pl.loop(1, nc)
    def _(k):
        f_copy(k).start()

    def e_copy(t):
        db, dc = lax.rem(b + lax.div(t, nc), nb), lax.rem(c + lax.rem(t, nc), nc)
        return copy(
            packed.at[db, pl.ds(pl.multiple_of(dc * slots, slots), slots)],
            eigrx.at[me],
            e_s.at[t],
            e_r.at[me],
            db,
            dc,
        )

    def o_copy(t):
        db, dc = lax.rem(b + lax.div(t, nc), nb), lax.rem(c + lax.rem(t, nc), nc)
        return copy(offsend.at[dc], offrx.at[me], o_s.at[t], o_r.at[me], db, dc)

    first = (n - 1) * FIRST // 32
    each = (n - 1) * EACH // (32 * (nc - 1))
    last = first + each * (nc - 1)

    @pl.loop(1, 1 + first)
    def _(t):
        e_copy(t).start()

    def p_copy(k):
        s = lax.rem(c - k + nc, nc)
        return copy(ppart.at[s], prx.at[c], p_s.at[k], p_r.at[c], b, s)

    @pl.loop(1, nc)
    def _(k):
        s = lax.rem(c - k + nc, nc)
        copy(feat, feat_all.at[s], f_s.at[k], f_r.at[s], b, s).wait_recv()
        kv, pv = block(feat_all[s])
        kbuf[s] = kv
        ppart[s] = pv
        p_copy(k).start()

        @pl.loop(0, each)
        def _(t):
            e_copy(1 + first + (k - 1) * each + t).start()

    @pl.loop(1, nc)
    def _(k):
        s = lax.rem(c + k, nc)
        copy(ppart.at[s], prx.at[s], p_s.at[k], p_r.at[s], b, s).wait_recv()

    pred = prx[0]
    for j in range(1, nc):
        pred = pred + prx[j]
    resid = unfold(pred) * sa - targ
    rs = resid * (sa / math.sqrt(rows_total))
    folded = fold(rs)
    rsend[...] = folded
    rrx[c] = folded

    def r_copy(k):
        return copy(rsend, rrx.at[c], r_s.at[k], r_r.at[c], b, lax.rem(c + k, nc))

    @pl.loop(1, nc)
    def _(k):
        r_copy(k).start()

    @pl.loop(1, n)
    def _(t):
        o_copy(t).start()

    @pl.loop(1 + last, n)
    def _(t):
        e_copy(t).start()

    res_out[...] = resid

    @pl.loop(1, nc)
    def _(k):
        s = lax.rem(c - k + nc, nc)
        copy(rsend, rrx.at[s], r_s.at[k], r_r.at[s], b, s).wait_recv()

    outs = res_out.shape[1]
    every = jnp.concatenate([unfold(rrx[j]) for j in range(nc)], axis=0)
    gt = (
        dot(every, kbuf[...].reshape(nc * rows, cdev), 0, 0) * sb_row
    )

    for j in range(nb):
        gsend[j] = gt[:, j * piece : (j + 1) * piece]

    def b_scatter(k, src, dst, ssem, rsem):
        d = lax.rem(b + k, nb)
        return copy(src.at[d], dst.at[b], ssem.at[k], rsem.at[b], d, c)

    def b_gather(k, src, dst, ssem, rsem):
        d = lax.rem(b + k, nb)
        return copy(src, dst.at[b], ssem.at[k], rsem.at[b], d, c)

    def b_wait(k, src, dst, ssem, rsem):
        d = lax.rem(b + k, nb)
        copy(src, dst.at[d], ssem.at[k], rsem.at[d], d, c).wait_recv()

    for k in range(1, nb):
        b_scatter(k, gsend, grx, g_s, g_r).start()
    grx[b] = gsend[b]

    def add_group(j):
        g = lax.rem(b - j + nb, nb) * nc

        @pl.loop(1 if j == 0 else 0, nc)
        def _(i):
            s = g + lax.rem(c - i + nc, nc)
            copy(offsend.at[0], offrx.at[s], o_s.at[i], o_r.at[s], b, c).wait_recv()
            copy(packed.at[0, pl.ds(0, slots)], eigrx.at[s], e_s.at[i], e_r.at[s], b, c).wait_recv()

        mark = offrx[g]
        for i in range(1, nc):
            mark = mark + offrx[g + i]
        sel = (
            lax.broadcasted_iota(jnp.int32, (cdev, nc * slots), 0) + 1 == mark.astype(jnp.int32)
        ).astype(jnp.float32).astype(jnp.bfloat16)
        part = pick(sel, eigrx[pl.ds(g, nc)].reshape(nc * slots, qb))
        ebar[...] = part if j == 0 else ebar[...] + part

    early = min(EARLY, nb)
    for j in range(early):
        add_group(j)

    for k in range(1, nb):
        b_wait(k, gown, grx, g_s, g_r)
    gsum = grx[0]
    for j in range(1, nb):
        gsum = gsum + grx[j]
    gown[...] = gsum
    gall[b] = gsum
    for k in range(1, nb):
        b_gather(k, gown, gall, ga_s, ga_r).start()
    for j in range(early, nb):
        add_group(j)
    for k in range(1, nb):
        b_wait(k, gown, gall, ga_s, ga_r)

    coeff = None
    for j in range(nb):
        part = dot(gall[j], ebar[j * piece : (j + 1) * piece], 1, 0)
        coeff = part if coeff is None else coeff + part
    og = outs // nc
    for j in range(nc):
        csend[j] = coeff[j * og : (j + 1) * og]

    def c_copy(k):
        d = lax.rem(c + k, nc)
        return copy(csend.at[d], crx.at[c], c_s.at[k], c_r.at[c], b, d)

    @pl.loop(1, nc)
    def _(k):
        c_copy(k).start()

    crx[c] = csend[c]

    @pl.loop(1, nc)
    def _(k):
        s = lax.rem(c - k + nc, nc)
        copy(csend.at[0], crx.at[s], c_s.at[k], c_r.at[s], b, s).wait_recv()

    csum = crx[0]
    for j in range(1, nc):
        csum = csum + crx[j]
    csum = csum * scale[b]
    cown[...] = csum
    call[c] = csum

    def ca_copy(k):
        return copy(cown, call.at[c], ca_s.at[k], ca_r.at[c], b, lax.rem(c + k, nc))

    @pl.loop(1, nc)
    def _(k):
        ca_copy(k).start()

    @pl.loop(1, nc)
    def _(k):
        s = lax.rem(c - k + nc, nc)
        copy(cown, call.at[s], ca_s.at[k], ca_r.at[s], b, s).wait_recv()

    scaled = jnp.concatenate([call[j] for j in range(nc)], axis=0)
    for j in range(nb):
        usend[j] = dot(scaled, ebar[j * piece : (j + 1) * piece], 1, 1)
    for k in range(1, nb):
        b_scatter(k, usend, urx, u_s, u_r).start()
    urx[b] = usend[b]
    for k in range(1, nb):
        b_wait(k, uown, urx, u_s, u_r)
    usum = urx[0]
    for j in range(1, nb):
        usum = usum + urx[j]
    usum = usum - gown[...]
    uown[...] = usum
    uall[b] = usum
    for k in range(1, nb):
        b_gather(k, uown, uall, ua_s, ua_r).start()
    for k in range(1, nb):
        b_wait(k, uown, uall, ua_s, ua_r)
    for j in range(nb):
        upd_out[:, j * piece : (j + 1) * piece] = uall[j]

    @pl.loop(1, nc)
    def _(k):
        f_copy(k).wait_send()
        p_copy(k).wait_send()
        r_copy(k).wait_send()
        c_copy(k).wait_send()
        ca_copy(k).wait_send()

    @pl.loop(1, n)
    def _(k):
        e_copy(k).wait_send()
        o_copy(k).wait_send()

    for k in range(1, nb):
        b_scatter(k, gsend, grx, g_s, g_r).wait_send()
        b_gather(k, gown, gall, ga_s, ga_r).wait_send()
        b_scatter(k, usend, urx, u_s, u_r).wait_send()
        b_gather(k, uown, uall, ua_s, ua_r).wait_send()


def per_device(
    pool_features,
    pool_targets,
    batch_index,
    centers,
    weights,
    eig_vectors,
    eig_scale,
    nys_owner,
    nys_offset,
):
    nb, nc = lax.axis_size("batch"), lax.axis_size("centers")
    n = nb * nc
    rows, dim = batch_index.shape[0], pool_features.shape[1]
    outs = pool_targets.shape[1]
    cdev = centers.shape[0]
    pts, q = eig_vectors.shape
    slots = max(2, 2 * pts // nc)
    qb, piece, og = q // nb, cdev // nb, outs // nc
    f32 = jnp.float32
    vm = pltpu.VMEM
    dma = pltpu.SemaphoreType.DMA
    spec = pl.BlockSpec(memory_space=pltpu.VMEM)
    pair = [dma((nc,)), dma((nc,))]
    every = [dma((n,)), dma((n,))]
    quad = [dma((nb,)), dma((nb,))]
    residual, update = pl.pallas_call(
        functools.partial(body, nb, nc),
        out_shape=(
            jax.ShapeDtypeStruct((rows, outs), f32),
            jax.ShapeDtypeStruct((outs, cdev), f32),
        ),
        in_specs=[spec] * 9,
        out_specs=(spec, spec),
        scratch_shapes=[
            vm((rows, dim), f32),
            vm((nc, rows, dim), f32),
            vm((nc, rows, cdev), f32),
            vm((nc, rows // 2, 2 * outs), f32),
            vm((nc, rows // 2, 2 * outs), f32),
            vm((rows // 2, 2 * outs), f32),
            vm((nc, rows // 2, 2 * outs), f32),
            vm((nb, nc * slots, qb), f32),
            vm((n, slots, qb), f32),
            vm((nc, 1, nc * slots), f32),
            vm((n, 1, nc * slots), f32),
            vm((cdev, qb), f32),
            vm((nb, outs, piece), f32),
            vm((nb, outs, piece), f32),
            vm((outs, piece), f32),
            vm((nb, outs, piece), f32),
            vm((nc, og, qb), f32),
            vm((nc, og, qb), f32),
            vm((og, qb), f32),
            vm((nc, og, qb), f32),
            vm((nb, outs, piece), f32),
            vm((nb, outs, piece), f32),
            vm((outs, piece), f32),
            vm((nb, outs, piece), f32),
        ]
        + pair * 3
        + every * 2
        + quad * 2
        + pair * 2
        + quad * 2,
        compiler_params=pltpu.CompilerParams(collective_id=0, has_side_effects=True),
    )(
        pool_features,
        pool_targets.T,
        batch_index[None, :],
        centers,
        weights.T,
        eig_vectors,
        eig_scale.reshape(nb, 1, qb),
        nys_owner.reshape(1, pts),
        nys_offset[None, :],
    )
    return (residual, update.T)


def solution(mesh):
    placed = (
        P(("batch", "centers"), None),
        P(("batch", "centers"), None),
        P(("batch", "centers")),
        P("centers", None),
        P("centers", None),
        P(("batch", "centers"), None),
        P(),
        P(("batch", "centers"), None),
        P(("batch", "centers")),
    )
    return jax.shard_map(
        per_device,
        mesh=mesh,
        in_specs=placed,
        out_specs=(P(("batch", "centers"), None), P("centers", None)),
        check_vma=False,
    )
```
